32 devices in a mesh: dp: 8 (over z, y), tensor: 4 (over x, core).
Axes of the slice: x: 2, y: 2, z: 4, core: 2. Of those that a mesh axis runs over, the one named last changes fastest.
Arguments:
- x_in: bfloat16 [1576, 768], P('dp'), may hold values from -6 to 6
- cotangent: bfloat16 [1576, 768], P('dp'), may hold values from -6 to 6
- routes: int32 [1576, 2], P('dp'), may hold values from 0 to 3, all different within a row; in each aligned block of 197 rows (0 to 196, 197 to 393, ...) at most 196 rows name the same one
- norm_gains: float32 [2, 768], P(None, 'dp'), may hold values from 0.5 to 1.5
- norm_biases: float32 [2, 768], P(None, 'dp'), may hold values from -1.5 to 1.5
- qkv_weight: float32 [3, 768, 768], P(None, 'dp', 'tensor'), may hold values from -0.21875 to 0.21875
- out_weight: float32 [768, 768], P('dp', 'tensor'), may hold values from -0.875 to 0.875
- router_weight: float32 [768, 4], P('dp'), may hold values from -0.21875 to 0.21875
- expert_up: float32 [8, 768, 1536], P('dp', None, 'tensor'), may hold values from -0.21875 to 0.21875
- expert_down: float32 [8, 768, 1536], P('dp', None, 'tensor'), may hold values from -0.109375 to 0.109375
- gains_mom: float32 [2, 768], P(None, 'dp'), may hold values from -120 to 120
- biases_mom: float32 [2, 768], P(None, 'dp'), may hold values from -120 to 120
- qkv_mom: float32 [3, 768, 768], P(None, 'dp', 'tensor'), may hold values from -12 to 12
- out_mom: float32 [768, 768], P('dp', 'tensor'), may hold values from -12 to 12
- router_mom: float32 [768, 4], P('dp'), may hold values from -3 to 3
- up_mom: float32 [8, 768, 1536], P('dp', None, 'tensor'), may hold values from -12 to 12
- down_mom: float32 [8, 768, 1536], P('dp', None, 'tensor'), may hold values from -24 to 24
Outputs:
- block_out: bfloat16 [1576, 768], P('dp')
- input_grad: bfloat16 [1576, 768], P('dp')
- gains_grad: float32 [2, 768], P(None, 'dp')
- biases_grad: float32 [2, 768], P(None, 'dp')
- qkv_grad: float32 [3, 768, 768], P(None, 'dp', 'tensor')
- out_grad: float32 [768, 768], P('dp', 'tensor')
- router_grad: float32 [768, 4], P('dp')
- up_grad: float32 [8, 768, 1536], P('dp', None, 'tensor')
- down_grad: float32 [8, 768, 1536], P('dp', None, 'tensor')
- new_gains: float32 [2, 768], P(None, 'dp')
- new_biases: float32 [2, 768], P(None, 'dp')
- new_qkv: float32 [3, 768, 768], P(None, 'dp', 'tensor')
- new_out: float32 [768, 768], P('dp', 'tensor')
- new_router: float32 [768, 4], P('dp')
- new_up: float32 [8, 768, 1536], P('dp', None, 'tensor')
- new_down: float32 [8, 768, 1536], P('dp', None, 'tensor')
- new_gains_mom: float32 [2, 768], P(None, 'dp')
- new_biases_mom: float32 [2, 768], P(None, 'dp')
- new_qkv_mom: float32 [3, 768, 768], P(None, 'dp', 'tensor')
- new_out_mom: float32 [768, 768], P('dp', 'tensor')
- new_router_mom: float32 [768, 4], P('dp')
- new_up_mom: float32 [8, 768, 1536], P('dp', None, 'tensor')
- new_down_mom: float32 [8, 768, 1536], P('dp', None, 'tensor')
The draws below stay inside these ranges and needn't reach their ends.
Inputs may be any that keep to these rules, and one draw needn't show every extreme that they name: Each token names two different experts. In the rows of one dp index no expert is named by more than 196 routes, a bound that some block reaches.
All inputs are finite; a program needn't handle non-finite values.
Results may differ from the reference program's by a relative error of at most 0.017.
Values may be sent and summed in bfloat16 or wider, within the bound.
No kernel may reach another device: no remote copies, remote signals or barrier semaphores. Data moves between devices by JAX's collectives and lax.ppermute only.
A program may use at most 128 MiB of HBM per device.

```python
import math
import jax
import jax.numpy as jnp
import numpy as np
from jax import lax

D = 768
HEADS = 12
DH = 64
HID = 3072
SEQ = 197
ESPLIT = 2
NS_STEPS = 5
EXPERTS = 4
ROWS = 197
TOKENS = 1576
CAP = 196
N_DP = 8
N_TENSOR = 4


def rising_momentum(key, salt):
    sub = jax.random.fold_in(key, salt)
    place = jnp.arange(D, dtype=jnp.float32) / jnp.float32(max(D - 1, 1))
    scale = 3.0 * jnp.power(10.0, place)
    noise = jnp.clip(jax.random.normal(sub, (2, D), jnp.float32), -4.0, 4.0)
    return (noise * scale[None, :]).astype(jnp.float32)


def draw_gains_mom(key, part):
    return rising_momentum(key, 7101)


def draw_biases_mom(key, part):
    return rising_momentum(key, 7202)


def block_levels(rng, shape, cuts, smallest, top_value):
    def one(dim, shards_of):
        heights = jax.random.uniform(jax.random.fold_in(jax.random.fold_in(rng, 6), dim), (shards_of,), jnp.float32, smallest / len(cuts), top_value / len(cuts))
        return jnp.repeat(jnp.exp(heights), shape[dim] // shards_of).reshape((-1,) + (1,) * (len(shape) - dim - 1))

    loudness = one(*cuts[0])
    for cut in cuts[1:]:
        loudness = loudness * one(*cut)
    return loudness


def shared_out(key, own, number, rows, amount, top, bound, skew):
    sequence = jax.random.permutation(key, amount)
    packed, ordinary = load_shares(amount, rows * top, bound, skew, True), load_shares(amount, rows * top, bound, skew, False)
    places = jnp.arange(amount)

    def named(sizes, rotation):
        used = int((sizes > 0).sum())
        fixed = max(1, used // 4)
        moved = fixed + (places - fixed + rotation * (used - fixed)) % max(1, amount - fixed)
        return jnp.zeros((amount,), jnp.int32).at[sequence[jnp.where(places < fixed, places, moved)]].set(jnp.asarray(sizes, jnp.int32))

    sizes = jnp.where(number % 4 == 0, named(packed, number // 4), named(ordinary, number - number // 4 - 1))
    mixed = jax.random.permutation(jax.random.fold_in(own, 3), amount)
    giver, taker = mixed[0:amount // 2 * 2:2], mixed[1:amount // 2 * 2:2]
    slack = jnp.minimum(sizes[giver] - 1, bound - sizes[taker]) // 2
    slack = jnp.where((giver == sequence[0]) | (taker == sequence[0]) | (sizes[taker] == 0), 0, jnp.maximum(slack, 0))
    moved = jax.random.randint(jax.random.fold_in(own, 4), (amount // 2,), 0, 1 << 20) % (slack + 1)
    sizes = sizes.at[giver].add(-moved).at[taker].add(moved)
    items = jnp.searchsorted(jnp.cumsum(sizes), jnp.arange(rows * top), side="right").astype(jnp.int32)
    listing = items.reshape(top, rows).T
    listing = listing[jax.random.permutation(jax.random.fold_in(own, 1), rows)]
    rotation = jax.random.randint(jax.random.fold_in(own, 2), (rows, 1), 0, top)
    return jnp.take_along_axis(listing, (jnp.arange(top)[None, :] + rotation) % top, axis=1)


def load_shares(number_of, total, limit, skew, full):
    loads = [(1 << 20) // math.isqrt(grade ** skew) + 1 for grade in range(1, number_of + 1)]
    largest = limit if full else min(limit, max(-(-total // number_of), total * loads[0] // sum(loads)))
    least = 1 if total - largest >= number_of - 1 else 0
    given, surplus = [largest] + [least] * (number_of - 1), total - largest - least * (number_of - 1)
    while surplus > 0:
        movable = [i for i in range(1, number_of) if given[i] < largest] or [i for i in range(1, number_of) if given[i] < limit]
        pool, remaining = sum([loads[i] for i in movable]), surplus
        for i in movable:
            more = min(limit - given[i], max(1, remaining * loads[i] // pool), surplus)
            given[i] = given[i] + more
            surplus = surplus - more
    return np.array(given)


def scatter_about(stream_key, extent, scale, bound, cuts=(), kind=jnp.bfloat16):
    entries = scale * jax.random.normal(stream_key, extent, jnp.float32)
    if cuts:
        entries = entries * block_levels(stream_key, extent, cuts, -0.22, 0.18)
    return jnp.clip(entries, -bound, bound).astype(kind)


def setup_inputs(seed: int = 0) -> dict:
    seeds = jax.random.split(jax.random.key(seed), 18)
    x_in = scatter_about(seeds[0], (TOKENS, D), 1.0, 6.0, ((0, 8),))
    cotangent = scatter_about(seeds[1], (TOKENS, D), 1.0, 6.0, ((0, 8),))
    routes_keys = jax.random.split(jax.random.fold_in(seeds[2], 1), TOKENS // ROWS)
    routes_turns = jax.random.permutation(jax.random.fold_in(seeds[2], 3), TOKENS // ROWS)
    routes = jax.vmap(lambda own, number: shared_out(jax.random.fold_in(seeds[2], 2), own, number, ROWS, EXPERTS, 2, CAP, 2))(routes_keys, routes_turns).reshape((TOKENS, 2))
    norm_gains = jnp.clip(1.0 + 0.1 * jax.random.normal(seeds[3], (2, D), jnp.float32), 0.5, 1.5)
    norm_biases = scatter_about(seeds[4], (2, D), 0.3, 1.5, ((1, 8),), jnp.float32)
    qkv_weight = scatter_about(seeds[5], (3, D, D), D ** -0.5, 0.21875, ((1, 8), (2, 4)), jnp.float32)
    out_weight = scatter_about(seeds[6], (D, D), (D // 16) ** -0.5, 0.875, ((0, 8), (1, 4)), jnp.float32)
    router_weight = scatter_about(seeds[7], (D, EXPERTS), D ** -0.5, 0.21875, ((0, 8),), jnp.float32)
    expert_up = scatter_about(seeds[8], (EXPERTS * ESPLIT, D, HID // ESPLIT), D ** -0.5, 0.21875, ((0, 8), (2, 4)), jnp.float32)
    expert_down = scatter_about(seeds[9], (EXPERTS * ESPLIT, D, HID // ESPLIT), HID ** -0.5, 0.109375, ((0, 8), (2, 4)), jnp.float32)
    gains_mom = draw_gains_mom(jax.random.fold_in(seeds[17], 71), 0)
    biases_mom = draw_biases_mom(jax.random.fold_in(seeds[17], 71), 0)
    qkv_mom = scatter_about(seeds[12], (3, D, D), 2.0, 12.0, ((1, 8), (2, 4)), jnp.float32)
    out_mom = scatter_about(seeds[13], (D, D), 2.0, 12.0, ((0, 8), (1, 4)), jnp.float32)
    router_mom = scatter_about(seeds[14], (D, EXPERTS), 0.5, 3.0, ((0, 8),), jnp.float32)
    up_mom = scatter_about(seeds[15], (EXPERTS * ESPLIT, D, HID // ESPLIT), 2.0, 12.0, ((0, 8), (2, 4)), jnp.float32)
    down_mom = scatter_about(seeds[16], (EXPERTS * ESPLIT, D, HID // ESPLIT), 4.0, 24.0, ((0, 8), (2, 4)), jnp.float32)
    return dict(x_in=x_in, cotangent=cotangent, routes=routes, norm_gains=norm_gains, norm_biases=norm_biases, qkv_weight=qkv_weight, out_weight=out_weight, router_weight=router_weight, expert_up=expert_up, expert_down=expert_down, gains_mom=gains_mom, biases_mom=biases_mom, qkv_mom=qkv_mom, out_mom=out_mom, router_mom=router_mom, up_mom=up_mom, down_mom=down_mom)


MOMENTUM = 0.95
MAT_RATE = 0.2
VEC_RATE = 0.1
COEF_A = 3.4445
COEF_B = -4.775
COEF_C = 2.0315
HIGHEST = lax.Precision.HIGHEST

def rounded(values):
    return lax.optimization_barrier(values.astype(jnp.bfloat16)).astype(jnp.float32)

def product(spec, left, right):
    return jnp.einsum(spec, left.astype(jnp.float32), right.astype(jnp.float32), precision=HIGHEST)

def cdf_part(values):
    return 0.5 * (1.0 + lax.erf(values * 0.7071067811865476))

def gelu_value(values):
    return values * cdf_part(values)

def gelu_slope(values):
    return cdf_part(values) + values * jnp.exp(-0.5 * values * values) * 0.3989422804014327

def norm_forward(values, gain_row, shift_row):
    center = values - lax.optimization_barrier(jnp.mean(values, axis=-1, keepdims=True))
    inverse = lax.rsqrt(lax.optimization_barrier(jnp.mean(center * center, axis=-1, keepdims=True)) + 1e-06)
    normal_hat = center * inverse
    return (normal_hat * gain_row + shift_row, normal_hat, inverse)

def norm_backward(upstream, normal_hat, inverse, gain_row):
    scaled = upstream * gain_row
    return inverse * (scaled - lax.optimization_barrier(jnp.mean(scaled, axis=-1, keepdims=True)) - normal_hat * lax.optimization_barrier(jnp.mean(scaled * normal_hat, axis=-1, keepdims=True)))

def newton_poly(gram):
    return COEF_B * gram + COEF_C * jnp.einsum('jqp,jpk->jqk', gram, gram, precision=HIGHEST)

def orthogonalize(moment):
    square = lax.optimization_barrier(jnp.sum(moment * moment, axis=(1, 2), keepdims=True))
    iterate = moment / (jnp.sqrt(square) + 1e-07)
    for step in range(NS_STEPS):
        gram = jnp.einsum('jrq,jrp->jqp', iterate, iterate, precision=HIGHEST)
        iterate = COEF_A * iterate + jnp.einsum('jrq,jqp->jrp', iterate, newton_poly(gram), precision=HIGHEST)
    return iterate

def muon_step(weight, moment, grad):
    fresh = MOMENTUM * moment + grad
    rate = MAT_RATE * max(1.0, weight.shape[1] / weight.shape[2]) ** 0.5
    return (weight - rate * orthogonalize(fresh), fresh)

def muon_mapped(weight, moment, grad):

    def single(items):
        new_weight, fresh = muon_step(items[0][None], items[1][None], items[2][None])
        return (new_weight[0], fresh[0])
    return lax.map(single, (weight, moment, grad))

def column_blocks(matrix):
    lead = matrix.shape[:-2]
    rows, cols = (matrix.shape[-2], matrix.shape[-1])
    split = matrix.reshape(lead + (rows, N_TENSOR, cols // N_TENSOR))
    moved = jnp.moveaxis(split, -2, -3)
    return moved.reshape((-1, rows, cols // N_TENSOR))

def from_blocks(blocks, shape):
    lead = tuple(shape[:-2])
    rows, cols = (shape[-2], shape[-1])
    split = blocks.reshape(lead + (N_TENSOR, rows, cols // N_TENSOR))
    return jnp.moveaxis(split, -3, -2).reshape(shape)

def vector_step(weight, moment, grad):
    fresh = MOMENTUM * moment + grad
    scale = jnp.sqrt(lax.optimization_barrier(jnp.mean(fresh * fresh, axis=-1, keepdims=True)) + 1e-05)
    return (weight - VEC_RATE * fresh / scale, fresh)

def reference(x_in, cotangent, routes, norm_gains, norm_biases, qkv_weight, out_weight, router_weight, expert_up, expert_down, gains_mom, biases_mom, qkv_mom, out_mom, router_mom, up_mom, down_mom):
    bf16 = jnp.bfloat16
    images = TOKENS // SEQ
    slots_all = EXPERTS * CAP
    blocks_per = ESPLIT * N_TENSOR
    block_cols = HID // blocks_per
    gain_full = rounded(norm_gains)
    shift_full = rounded(norm_biases)
    weight_qkv = qkv_weight.astype(bf16)
    weight_out = out_weight.astype(bf16)
    weight_route = router_weight.astype(bf16)
    up_blocks = column_blocks(expert_up).astype(bf16).reshape(EXPERTS, blocks_per, D, block_cols)
    down_blocks = column_blocks(expert_down).astype(bf16).reshape(EXPERTS, blocks_per, D, block_cols)
    inputs = x_in.astype(jnp.float32)
    normed_a, hat_a, scale_a = norm_forward(inputs, gain_full[0], shift_full[0])
    normed_a_bf = normed_a.astype(bf16)
    projected = product('rd,jde->jre', normed_a_bf, weight_qkv).astype(bf16)
    split_heads = projected.reshape(3, images, SEQ, HEADS, DH)
    query, keys, values = (split_heads[0], split_heads[1], split_heads[2])
    score_scale = DH ** (-0.5)
    scores = product('ishd,ithd->ihst', query, keys) * score_scale
    log_total = jnp.log(lax.optimization_barrier(jnp.sum(jnp.exp(scores), axis=-1, keepdims=True)))
    probs_att = jnp.exp(scores - log_total)
    weights_bf = probs_att.astype(bf16)
    context = product('ihst,ithd->ishd', weights_bf, values).astype(bf16)
    context_rows = context.reshape(TOKENS, D)
    middle = inputs + product('rq,dq->rd', context_rows, weight_out)
    normed_b, hat_b, scale_b = norm_forward(middle, gain_full[1], shift_full[1])
    normed_b_bf = normed_b.astype(bf16)
    logits = product('rd,de->re', normed_b_bf, weight_route)
    expo = jnp.exp(logits)
    probs = expo / lax.optimization_barrier(jnp.sum(expo, axis=-1, keepdims=True))
    chosen = (routes[:, :, None] == jnp.arange(EXPERTS, dtype=jnp.int32)[None, None, :]).astype(jnp.float32)
    picked = lax.optimization_barrier(jnp.sum(chosen * probs[:, None, :], axis=-1))
    picked_total = lax.optimization_barrier(jnp.sum(picked, axis=-1, keepdims=True))
    gates = picked / picked_total
    flat_routes = routes.reshape(N_DP, 2 * ROWS)
    hot_counts = (flat_routes[:, :, None] == jnp.arange(EXPERTS, dtype=jnp.int32)[None, None, :]).astype(jnp.int32)
    earlier = jnp.cumsum(hot_counts, axis=1) - hot_counts
    position = lax.optimization_barrier(jnp.sum(earlier * hot_counts, axis=2))
    slot_index = (flat_routes * CAP + position).astype(jnp.int32)
    device_index = jnp.broadcast_to(jnp.arange(N_DP, dtype=jnp.int32)[:, None], slot_index.shape)
    repeated = jnp.repeat(normed_b_bf.reshape(N_DP, ROWS, D), 2, axis=1)
    buffers = jnp.zeros((N_DP, slots_all, D), bf16).at[device_index, slot_index].set(repeated)

    def by_expert(array):
        return array.reshape(N_DP, EXPERTS, CAP, D).transpose(1, 0, 2, 3).reshape(EXPERTS, N_DP * CAP, D)

    def by_source(array):
        return array.reshape(EXPERTS, N_DP, CAP, D).transpose(1, 0, 2, 3).reshape(N_DP, slots_all, D)

    def expert_forward(items):
        token_block, up_here, down_here = items
        pre_hidden = product('md,kdb->kmb', token_block, up_here)
        hidden_bf = gelu_value(pre_hidden).astype(bf16)
        return lax.optimization_barrier(jnp.sum(rounded(product('kmb,kdb->kmd', hidden_bf, down_here)), axis=0))
    expert_out = lax.map(expert_forward, (by_expert(buffers), up_blocks, down_blocks))
    slot_values = by_source(expert_out)
    per_route = slot_values[device_index, slot_index].reshape(TOKENS, 2, D)
    mixed = lax.optimization_barrier(jnp.sum(gates[:, :, None] * per_route, axis=1))
    block_out = (middle + mixed).astype(bf16)
    upstream = cotangent.astype(jnp.float32)
    gate_grad = lax.optimization_barrier(jnp.sum(upstream[:, None, :] * per_route, axis=-1))
    route_values = (gates[:, :, None] * upstream[:, None, :]).astype(bf16).reshape(N_DP, 2 * ROWS, D)
    grad_buffers = jnp.zeros((N_DP, slots_all, D), bf16).at[device_index, slot_index].set(route_values)

    def expert_backward(items):
        token_block, grad_block, up_here, down_here = items
        pre_hidden = product('md,kdb->kmb', token_block, up_here)
        hidden_bf = gelu_value(pre_hidden).astype(bf16)
        hidden_grad = product('md,kdb->kmb', grad_block, down_here)
        down_grad_here = product('md,kmb->kdb', grad_block, hidden_bf)
        pre_grad_bf = (hidden_grad * gelu_slope(pre_hidden)).astype(bf16)
        up_grad_here = product('md,kmb->kdb', token_block, pre_grad_bf)
        token_grad = lax.optimization_barrier(jnp.sum(rounded(product('kmb,kdb->kmd', pre_grad_bf, up_here)), axis=0))
        return (up_grad_here, down_grad_here, token_grad)
    up_grad_blocks, down_grad_blocks, token_grads = lax.map(expert_backward, (by_expert(buffers), by_expert(grad_buffers), up_blocks, down_blocks))
    slot_back = by_source(token_grads)
    expert_input_grad = lax.optimization_barrier(jnp.sum(slot_back[device_index, slot_index].reshape(TOKENS, 2, D), axis=1))
    weighted = lax.optimization_barrier(jnp.sum(gate_grad * gates, axis=-1, keepdims=True))
    picked_grad = (gate_grad - weighted) / picked_total
    prob_grad = lax.optimization_barrier(jnp.sum(chosen * picked_grad[:, :, None], axis=1))
    logit_grad = probs * (prob_grad - lax.optimization_barrier(jnp.sum(probs * prob_grad, axis=-1, keepdims=True)))
    router_grad = product('rd,re->de', normed_b_bf, logit_grad)
    normed_b_grad = expert_input_grad + product('re,de->rd', logit_grad, weight_route)
    gain_b_grad = lax.optimization_barrier(jnp.sum(normed_b_grad * hat_b, axis=0))
    shift_b_grad = lax.optimization_barrier(jnp.sum(normed_b_grad, axis=0))
    middle_grad = upstream + norm_backward(normed_b_grad, hat_b, scale_b, gain_full[1])
    middle_grad_bf = middle_grad.astype(bf16)
    context_grad = product('rd,dq->rq', middle_grad_bf, weight_out).astype(bf16)
    out_grad = product('rd,rq->dq', middle_grad_bf, context_rows)
    context_grad4 = context_grad.reshape(images, SEQ, HEADS, DH)
    value_grad = product('ihst,ishd->ithd', weights_bf, context_grad4).astype(bf16)
    prob_grad_att = product('ishd,ithd->ihst', context_grad4, values)
    row_dot = jnp.transpose(lax.optimization_barrier(jnp.sum(context_grad4.astype(jnp.float32) * context.astype(jnp.float32), axis=-1)), (0, 2, 1))[..., None]
    score_grad = (probs_att * (prob_grad_att - row_dot) * score_scale).astype(bf16)
    query_grad = product('ihst,ithd->ishd', score_grad, keys).astype(bf16)
    key_grad = product('ihst,ishd->ithd', score_grad, query).astype(bf16)
    projected_grad = jnp.stack([query_grad, key_grad, value_grad]).reshape(3, TOKENS, D)
    qkv_grad = product('rd,jre->jde', normed_a_bf, projected_grad)
    normed_a_grad = product('jre,jde->rd', projected_grad, weight_qkv)
    gain_a_grad = lax.optimization_barrier(jnp.sum(normed_a_grad * hat_a, axis=0))
    shift_a_grad = lax.optimization_barrier(jnp.sum(normed_a_grad, axis=0))
    input_grad = (middle_grad + norm_backward(normed_a_grad, hat_a, scale_a, gain_full[0])).astype(bf16)
    gains_grad = jnp.stack([gain_a_grad, gain_b_grad])
    biases_grad = jnp.stack([shift_a_grad, shift_b_grad])
    up_grad = from_blocks(up_grad_blocks.reshape(EXPERTS * blocks_per, D, block_cols), expert_up.shape)
    down_grad = from_blocks(down_grad_blocks.reshape(EXPERTS * blocks_per, D, block_cols), expert_down.shape)
    new_gains, new_gains_mom = vector_step(norm_gains, gains_mom, gains_grad)
    new_biases, new_biases_mom = vector_step(norm_biases, biases_mom, biases_grad)
    qkv_new_b, qkv_mom_b = muon_step(column_blocks(qkv_weight), column_blocks(qkv_mom), column_blocks(qkv_grad))
    out_new_b, out_mom_b = muon_step(column_blocks(out_weight), column_blocks(out_mom), column_blocks(out_grad))
    router_new_b, router_mom_b = muon_step(router_weight[None], router_mom[None], router_grad[None])
    up_new_b, up_mom_b = muon_mapped(column_blocks(expert_up), column_blocks(up_mom), column_blocks(up_grad))
    down_new_b, down_mom_b = muon_mapped(column_blocks(expert_down), column_blocks(down_mom), column_blocks(down_grad))
    new_qkv = from_blocks(qkv_new_b, qkv_weight.shape)
    new_qkv_mom = from_blocks(qkv_mom_b, qkv_weight.shape)
    new_out = from_blocks(out_new_b, out_weight.shape)
    new_out_mom = from_blocks(out_mom_b, out_weight.shape)
    new_up = from_blocks(up_new_b, expert_up.shape)
    new_up_mom = from_blocks(up_mom_b, expert_up.shape)
    new_down = from_blocks(down_new_b, expert_down.shape)
    new_down_mom = from_blocks(down_mom_b, expert_down.shape)
    return (block_out, input_grad, gains_grad, biases_grad, qkv_grad, out_grad, router_grad, up_grad, down_grad, new_gains, new_biases, new_qkv, new_out, router_new_b[0], new_up, new_down, new_gains_mom, new_biases_mom, new_qkv_mom, new_out_mom, router_mom_b[0], new_up_mom, new_down_mom)
```

```python
import jax
import jax.numpy as jnp
from jax import lax
from jax.sharding import PartitionSpec as P

D = 768
DH = 64
SEQ = 197
NS_STEPS = 5


MOMENTUM = 0.95
MAT_RATE = 0.2
VEC_RATE = 0.1
COEF_A = 3.4445
COEF_B = -4.775
COEF_C = 2.0315
HIGHEST = lax.Precision.HIGHEST


def cdf_part(values):
    return 0.5 * (1.0 + lax.erf(values * 0.7071067811865476))


def gelu_value(values):
    return values * cdf_part(values)


def gelu_slope(values):
    return cdf_part(values) + values * jnp.exp(-0.5 * values * values) * 0.3989422804014327


def norm_forward(values, gain_row, shift_row):
    center = values - jnp.mean(values, axis=-1, keepdims=True)
    inverse = lax.rsqrt(jnp.mean(center * center, axis=-1, keepdims=True) + 1e-06)
    normal_hat = center * inverse
    return (normal_hat * gain_row + shift_row, normal_hat, inverse)


def norm_backward(upstream, normal_hat, inverse, gain_row):
    scaled = upstream * gain_row
    return inverse * (
        scaled
        - jnp.mean(scaled, axis=-1, keepdims=True)
        - normal_hat * jnp.mean(scaled * normal_hat, axis=-1, keepdims=True)
    )


def newton_poly(gram):
    return COEF_B * gram + COEF_C * jnp.einsum("jqp,jpk->jqk", gram, gram, precision=HIGHEST)


def newton_update(iterate, gram):
    return COEF_A * iterate + jnp.einsum(
        "jrq,jqp->jrp", iterate, newton_poly(gram), precision=HIGHEST
    )


def orthogonalize(moment):
    square = jnp.sum(moment * moment, axis=(1, 2), keepdims=True)
    iterate = moment / (jnp.sqrt(square) + 1e-07)
    for step in range(NS_STEPS):
        gram = jnp.einsum("jrq,jrp->jqp", iterate, iterate, precision=HIGHEST)
        iterate = newton_update(iterate, gram)
    return iterate


BF16 = jnp.bfloat16
F32 = jnp.float32


def hop(array, axis, mask):
    return lax.ppermute(array, axis, [(k, k ^ mask) for k in range(lax.axis_size(axis))])


def join(first, second, axis=0):
    return jnp.concatenate([first, second], axis=axis)


def line_gather(block, bits):
    blocks = block[None]
    for bit in reversed(range(bits)):
        blocks = join(blocks, hop(blocks, "dp", 2 << bit))
    return blocks


def line_order(bits):
    order = [0]
    for bit in reversed(range(bits)):
        order = order + [k | (1 << bit) for k in order]
    return order


def line_reduce(blocks, bits):
    for bit in range(bits):
        half = blocks.shape[0] // 2
        arrived = hop(blocks[half:].astype(BF16), "dp", 2 << bit)
        blocks = blocks[:half].astype(F32) + arrived.astype(F32)
    return blocks[0]


def settle(values):
    return lax.optimization_barrier(values.astype(BF16))


def swap_sum(values, axis, mask):
    own = settle(values)
    return own.astype(F32) + hop(own, axis, mask).astype(F32)


def pieces(values):
    high = lax.reduce_precision(values, 8, 7)
    rest = values - high
    middle = lax.reduce_precision(rest, 8, 7)
    return [high.astype(BF16), middle.astype(BF16), (rest - middle).astype(BF16)]


def dot_high(spec, left, right):
    return jnp.einsum(spec, left, right, precision=HIGHEST)


def polar_factor(gram):
    size = gram.shape[-1]
    eye = jnp.eye(size, dtype=F32)
    norm = jnp.sqrt(jnp.sum(gram * eye, axis=(-2, -1), keepdims=True)) + 1e-07
    gram = gram / (norm * norm)
    total = None
    for step in range(NS_STEPS):
        factor = (
            COEF_A * eye + COEF_B * gram + COEF_C * dot_high("...ij,...jk->...ik", gram, gram)
        )
        total = factor if total is None else dot_high("...ij,...jk->...ik", total, factor)
        if step < NS_STEPS - 1:
            gram = dot_high(
                "...ij,...jk->...ik", dot_high("...ij,...jk->...ik", factor, gram), factor
            )
    return total / norm


def body_lines(
    x_in,
    cotangent,
    routes,
    norm_gains,
    norm_biases,
    qkv_weight,
    out_weight,
    router_weight,
    expert_up,
    expert_down,
    gains_mom,
    biases_mom,
    qkv_mom,
    out_mom,
    router_mom,
    up_mom,
    down_mom,
):
    token_count, width = x_in.shape
    images = token_count // SEQ
    experts = router_weight.shape[1]
    head_cols = qkv_weight.shape[2]
    heads_here = head_cols // DH
    rows_here = qkv_weight.shape[1]
    dp_count = lax.axis_size("dp")
    line_count = dp_count // 2
    bits = line_count.bit_length() - 1
    order = line_order(bits)
    me = lax.axis_index("dp")
    line_me = me // 2
    tensor_me = lax.axis_index("tensor")
    core = tensor_me % 2
    half = width // 2
    mine_at = core * half
    other_at = half - mine_at

    def mine(array):
        return lax.dynamic_slice_in_dim(array, mine_at, half, axis=array.ndim - 1)

    def other(array):
        return lax.dynamic_slice_in_dim(array, other_at, half, axis=array.ndim - 1)

    def turned(array, axis):
        return join(
            lax.dynamic_slice_in_dim(array, mine_at, half, axis=axis),
            lax.dynamic_slice_in_dim(array, other_at, half, axis=axis),
            axis,
        )

    def unturned(first, second, axis):
        return jnp.where(core == 0, join(first, second, axis), join(second, first, axis))

    small = jnp.concatenate([norm_gains, norm_biases, router_weight.T], axis=0)
    small_mom = jnp.concatenate([gains_mom, biases_mom, router_mom.T], axis=0)
    small_rows = small.shape[0]
    matrices = jnp.concatenate(
        [qkv_weight[0], qkv_weight[1], qkv_weight[2], out_weight], axis=1
    ).astype(BF16)
    packed_cols = matrices.shape[1]
    extra_rows = -(-small_rows * rows_here // packed_cols)

    def as_rows(values):
        flat = values.reshape(-1)
        flat = jnp.pad(flat, (0, extra_rows * packed_cols - flat.shape[0]))
        return flat.reshape(extra_rows, packed_cols)

    packed = jnp.concatenate(
        [matrices, as_rows(small.astype(BF16))] + [as_rows(v) for v in pieces(small_mom)], axis=0
    )
    packed = jnp.pad(packed, ((0, -packed.shape[0] % 8), (0, 0)))
    gathered = packed[None]
    offsets = [0]
    for bit in reversed(range(1, bits)):
        gathered = join(gathered, hop(gathered, "dp", 2 << bit))
        offsets = offsets + [k | (2 << bit) for k in offsets]
    arrived = hop(gathered, "dp", 2)
    side_a = hop(gathered, "dp", 1)
    side_b = hop(arrived, "dp", 1)
    gathered = jnp.concatenate([gathered, arrived, side_a, side_b], axis=0)
    offsets = offsets + [k | 2 for k in offsets]
    offsets = offsets + [k | 1 for k in offsets]
    place = [offsets.index(k) for k in range(dp_count)]
    place_table = jnp.asarray(place, dtype=jnp.int32)
    in_order = jnp.take(place_table, me ^ jnp.arange(dp_count, dtype=jnp.int32))
    gathered = jnp.take(gathered, in_order, axis=0)
    weights_full = gathered[:, :rows_here].reshape(width, packed_cols)

    def small_full(at):
        block = gathered[:, at : at + extra_rows].reshape(dp_count, -1)
        block = block[:, : small_rows * rows_here].astype(F32)
        return (
            block.reshape(dp_count, small_rows, rows_here)
            .transpose(1, 0, 2)
            .reshape(small_rows, width)
        )

    params = small_full(rows_here)
    small_mom_full = (
        small_full(rows_here + extra_rows) + small_full(rows_here + 2 * extra_rows)
    ) + small_full(rows_here + 3 * extra_rows)
    gain_full, shift_full, route_rows = params[0:2], params[2:4], params[4:]
    weight_qkv = weights_full[:, : 3 * head_cols]
    weight_out = weights_full[:, 3 * head_cols :]

    pair_out = jnp.stack([weight_out, hop(weight_out, "tensor", 2)])
    quad_out = jnp.concatenate([pair_out, hop(pair_out, "tensor", 1)], axis=0)
    tensor_place = jnp.asarray([0, 2, 1, 3], dtype=jnp.int32)
    tensor_order = jnp.take(tensor_place, tensor_me ^ jnp.arange(4, dtype=jnp.int32))
    weight_out_all = jnp.take(quad_out, tensor_order, axis=0)

    inputs = x_in.astype(F32)
    normed_a, hat_a, scale_a = norm_forward(inputs, gain_full[0], shift_full[0])
    normed_a_bf = normed_a.astype(BF16)
    projected = jnp.dot(normed_a_bf, weight_qkv, preferred_element_type=F32).astype(BF16)
    split_heads = projected.reshape(images, SEQ, 3, heads_here, DH)
    query, keys, values = (split_heads[:, :, 0], split_heads[:, :, 1], split_heads[:, :, 2])
    score_scale = DH ** (-0.5)
    scores = jnp.einsum("ishd,ithd->ihst", query, keys, preferred_element_type=F32) * score_scale
    log_total = jnp.log(jnp.sum(jnp.exp(scores), axis=-1, keepdims=True))
    probs_att = jnp.exp(scores - log_total)
    weights_bf = probs_att.astype(BF16)
    context = jnp.einsum("ihst,ithd->ishd", weights_bf, values, preferred_element_type=F32).astype(
        BF16
    )
    context_rows = context.reshape(token_count, head_cols)
    pair_ctx = jnp.stack([context_rows, hop(context_rows, "tensor", 2)])
    quad_ctx = jnp.concatenate([pair_ctx, hop(pair_ctx, "tensor", 1)], axis=0)
    context_all = jnp.take(quad_ctx, tensor_order, axis=0)
    attended = jnp.einsum("hrq,hdq->rd", context_all, weight_out_all, preferred_element_type=F32)
    middle = inputs + attended
    normed_b, hat_b, scale_b = norm_forward(middle, gain_full[1], shift_full[1])
    normed_b_bf = settle(normed_b)

    def route_probs(rows, table):
        logits = jnp.einsum("rd,ed->re", rows, table, preferred_element_type=F32)
        expo = jnp.exp(logits)
        return expo / jnp.sum(expo, axis=-1, keepdims=True)

    route_bf = route_rows.astype(BF16)
    probs = route_probs(normed_b_bf, route_bf)
    ids = jnp.arange(experts, dtype=jnp.int32)[None, None, :]
    chosen = (routes[:, :, None] == ids).astype(F32)
    picked = jnp.sum(chosen * probs[:, None, :], axis=-1)
    picked_total = jnp.sum(picked, axis=-1, keepdims=True)
    gates = picked / picked_total

    padded = -(-(token_count + 2 * experts) // 16) * 16
    pad_rows = padded - token_count

    def pad(array):
        return jnp.pad(array, ((0, pad_rows), (0, 0)))

    up_turned = turned(expert_up[0], 0).astype(BF16)
    down_turned = turned(expert_down[0], 0).astype(BF16)
    up_pair = join(up_turned, hop(up_turned, "dp", 1), 1)
    down_pair = join(down_turned, hop(down_turned, "dp", 1), 1)
    block_cols = up_turned.shape[1]

    early = jnp.stack([pad(cotangent), pad(x_in)])
    early_line = line_gather(mine(early), bits)
    early_rest = hop(early_line[1:], "tensor", 1)
    early_other = join(other(early)[None], early_rest)
    grads_line = join(early_line[:, 0], early_other[:, 0], 2)
    inputs_line = unturned(early_line[:, 1], early_other[:, 1], 2)
    normed_line = norm_forward(inputs_line.astype(F32), gain_full[0], shift_full[0])[0].astype(BF16)
    row_valid = (jnp.arange(padded) < token_count)[None, :, None]
    normed_line = jnp.where(row_valid, normed_line, 0).reshape(line_count * padded, width)
    route_pad = jnp.pad(routes, ((0, pad_rows), (0, 0)), constant_values=-1)
    routes_line = line_gather(route_pad.T, bits)
    routes_line = routes_line.transpose(0, 2, 1).reshape(line_count * padded, 2)

    moms = jnp.concatenate([qkv_mom, out_mom[None]], axis=0)
    if line_count > 4:
        moms = jnp.pad(moms, ((0, line_count - 4), (0, 0), (0, 0)))
    mom_pair = jnp.stack([moms, hop(moms, "dp", 1)], axis=1)

    def to_owner(stack):
        got = [lax.dynamic_index_in_dim(stack, line_me, 0, keepdims=False)]
        for k in range(1, line_count):
            chunk = lax.dynamic_index_in_dim(stack, line_me ^ k, 0, keepdims=False)
            got.append(hop(chunk, "dp", 2 * k))
        return jnp.stack(got)

    owned_mom = to_owner(mom_pair).reshape(dp_count, rows_here, head_cols)
    owned_mom = jnp.take(owned_mom, me ^ jnp.arange(dp_count, dtype=jnp.int32), axis=0)
    owned_mom = owned_mom.reshape(width, head_cols)

    tokens_mine = line_gather(mine(pad(normed_b_bf)), bits)
    tokens_other = join(other(pad(normed_b_bf))[None], hop(tokens_mine[1:], "tensor", 1))
    tokens = join(tokens_mine, tokens_other, 2).reshape(line_count * padded, width)
    grads = grads_line.reshape(line_count * padded, width)
    line_probs = route_probs(tokens, turned(route_bf, 1))
    first = (routes_line[:, 0:1] == ids[0]).astype(F32)
    second = (routes_line[:, 1:2] == ids[0]).astype(F32)
    both = first + second
    here = (jnp.arange(experts, dtype=jnp.int32) == line_me).astype(F32)[None, :]
    hit = jnp.sum(both * here, axis=-1, keepdims=True) > 0
    gate_here = jnp.where(
        hit,
        jnp.sum(line_probs * here, axis=-1, keepdims=True)
        / jnp.sum(line_probs * both, axis=-1, keepdims=True),
        0.0,
    )
    pre_hidden = jnp.dot(tokens, up_pair, preferred_element_type=F32)
    hidden_bf = gelu_value(pre_hidden).astype(BF16)
    expert_part = jnp.einsum("mb,db->md", hidden_bf, down_pair, preferred_element_type=F32)
    mixed_part = (expert_part * gate_here).reshape(line_count, padded, width)
    grads_f32 = grads.astype(F32)
    gate_dot = jnp.sum((grads_f32 * expert_part).reshape(line_count, padded, width), axis=-1)
    grads_bf = (grads_f32 * gate_here).astype(BF16)
    hidden_grad = jnp.einsum("md,db->mb", grads_bf, down_pair, preferred_element_type=F32)
    pre_grad_bf = (hidden_grad * gelu_slope(pre_hidden)).astype(BF16)
    token_part = jnp.einsum("mb,db->md", pre_grad_bf, up_pair, preferred_element_type=F32)
    token_part = token_part.reshape(line_count, padded, width)

    def home(part_mine, part_other):
        arrived = hop(part_other.astype(BF16), "tensor", 1)
        return line_reduce(part_mine.astype(F32) + arrived.astype(F32), bits)

    high, low = pieces(gate_dot)[0:2]
    row_id = jnp.arange(padded)[None, :, None]
    spread = jnp.zeros((line_count, 1, half - padded), BF16)
    high = join(high[:, None, :], spread, 2)
    low = join(low[:, None, :], spread, 2)
    part_mine = token_part[:, :, :half].astype(BF16)
    part_mine = jnp.where(row_id == token_count + 2 * line_me, high, part_mine)
    part_mine = jnp.where(row_id == token_count + 2 * line_me + 1, low, part_mine)
    reduced = home(part_mine, token_part[:, :, half:])
    reduced = swap_sum(reduced, "tensor", 2)
    gate_rows = reduced[token_count : token_count + 2 * experts].reshape(experts, 2, half)
    gate_rows = gate_rows[:, 0] + gate_rows[:, 1]
    high, low = pieces(gate_rows)[0:2]
    back_pack = jnp.concatenate(
        [reduced[:token_count].astype(BF16), high, low], axis=0
    )
    back_pack = lax.optimization_barrier(back_pack)
    back_other = hop(back_pack, "tensor", 1)
    expert_input_grad = unturned(back_pack[:token_count], back_other[:token_count], 1).astype(F32)

    def two_rows(array):
        high_rows = array[token_count : token_count + experts].astype(F32)
        return high_rows + array[token_count + experts :].astype(F32)

    gate_grad = (two_rows(back_pack) + two_rows(back_other))[:, :token_count].T

    up_both = jnp.einsum("md,mb->db", tokens, pre_grad_bf, preferred_element_type=F32)
    down_both = jnp.einsum("md,mb->db", grads_bf, hidden_bf, preferred_element_type=F32)

    def pair_sum(both_blocks):
        arrived = hop(both_blocks[:, block_cols:].astype(BF16), "dp", 1)
        total = both_blocks[:, :block_cols] + arrived.astype(F32)
        return unturned(total[:half], total[half:], 0)

    up_grad_block = pair_sum(up_both)
    down_grad_block = pair_sum(down_both)

    mixed = home(mixed_part[:, :, :half], mixed_part[:, :, half:])[:token_count]
    mixed = settle(swap_sum(mixed, "tensor", 2))
    mixed = unturned(mixed, hop(mixed, "tensor", 1), 1).astype(F32)
    block_out = (middle + mixed).astype(BF16)

    upstream = cotangent.astype(F32)
    chosen_any = jnp.sum(chosen, axis=1)
    gates_any = jnp.sum(chosen * gates[:, :, None], axis=1)
    weighted = jnp.sum(gates_any * gate_grad, axis=-1, keepdims=True)
    prob_grad = chosen_any * (gate_grad - weighted) / picked_total
    logit_grad = probs * (prob_grad - jnp.sum(probs * prob_grad, axis=-1, keepdims=True))
    route_grad_part = dot_high("re,rd->ed", logit_grad, normed_b_bf.astype(F32))
    normed_b_grad = expert_input_grad + dot_high("re,ed->rd", logit_grad, route_rows)
    gain_b_grad = jnp.sum(normed_b_grad * hat_b, axis=0)
    shift_b_grad = jnp.sum(normed_b_grad, axis=0)
    middle_grad = upstream + norm_backward(normed_b_grad, hat_b, scale_b, gain_full[1])
    middle_grad_bf = middle_grad.astype(BF16)

    context_grad = jnp.dot(middle_grad_bf, weight_out, preferred_element_type=F32).astype(BF16)
    out_grad_part = jnp.einsum(
        "rd,rq->dq", middle_grad_bf, context_rows, preferred_element_type=F32
    )
    for bit in range(bits):
        senders = [
            k
            for k in range(dp_count)
            if ((k // 2) ^ 3) % (1 << bit) == 0 and ((k // 2) ^ 3) >> bit & 1
        ]
        pairs = [(k, k ^ (2 << bit)) for k in senders]
        arrived = lax.ppermute(out_grad_part.astype(BF16), "dp", pairs)
        out_grad_part = out_grad_part + arrived.astype(F32)
    context_grad4 = context_grad.reshape(images, SEQ, heads_here, DH)
    value_grad = jnp.einsum(
        "ihst,ishd->ithd", weights_bf, context_grad4, preferred_element_type=F32
    ).astype(BF16)
    prob_grad_att = jnp.einsum(
        "ishd,ithd->ihst", context_grad4, values, preferred_element_type=F32
    )
    row_dot = jnp.einsum("ishd,ishd->ihs", context_grad4, context, preferred_element_type=F32)[
        ..., None
    ]
    score_grad = (probs_att * (prob_grad_att - row_dot) * score_scale).astype(BF16)
    query_grad = jnp.einsum("ihst,ithd->ishd", score_grad, keys, preferred_element_type=F32)
    key_grad = jnp.einsum("ihst,ishd->ithd", score_grad, query, preferred_element_type=F32)
    projected_grad = [
        piece.astype(BF16).reshape(token_count, head_cols)
        for piece in (query_grad, key_grad, value_grad)
    ]

    sent_grad = jnp.stack(
        [pad(piece) for piece in projected_grad]
        + [jnp.zeros((padded, head_cols), BF16)] * (line_count - 3)
    )
    owned_rows = to_owner(sent_grad)
    owned_rows = jnp.stack([owned_rows[k] for k in order]).reshape(-1, head_cols)
    owned_grad = jnp.einsum("rd,re->de", normed_line, owned_rows, preferred_element_type=F32)
    owned_grad = jnp.where(line_me == 3, out_grad_part, owned_grad)
    owned_grad = swap_sum(owned_grad, "dp", 1)
    owned_fresh = MOMENTUM * owned_mom + owned_grad
    factor = polar_factor(dot_high("rq,rp->qp", owned_fresh, owned_fresh))
    iterate = dot_high("rq,qp->rp", owned_fresh, factor)
    answer = jnp.stack([owned_grad.astype(BF16), iterate.astype(BF16)])
    answer = answer.reshape(2, line_count, 2, rows_here, head_cols)
    answer = lax.dynamic_index_in_dim(answer, me % 2, 2, keepdims=False).transpose(1, 0, 2, 3)
    answers = to_owner(answer)
    answers = jnp.take(answers, line_me ^ jnp.arange(4, dtype=jnp.int32), axis=0).astype(F32)
    attn_grad, attn_iterate = answers[:, 0], answers[:, 1]

    normed_a_part = jnp.dot(
        jnp.concatenate(projected_grad, axis=1), weight_qkv.T, preferred_element_type=F32
    )
    normed_a_half = mine(normed_a_part) + hop(
        other(normed_a_part).astype(BF16), "tensor", 1
    ).astype(F32)
    normed_a_half = settle(swap_sum(normed_a_half, "tensor", 2))
    normed_a_grad = unturned(normed_a_half, hop(normed_a_half, "tensor", 1), 1).astype(F32)
    gain_a_grad = jnp.sum(normed_a_grad * hat_a, axis=0)
    shift_a_grad = jnp.sum(normed_a_grad, axis=0)
    input_grad = (middle_grad + norm_backward(normed_a_grad, hat_a, scale_a, gain_full[0])).astype(
        BF16
    )

    small_grad = jnp.concatenate(
        [
            jnp.stack([gain_a_grad, gain_b_grad, shift_a_grad, shift_b_grad]),
            route_grad_part,
        ],
        axis=0,
    )
    for bit in range(dp_count.bit_length() - 1):
        small_grad = small_grad + hop(small_grad, "dp", 1 << bit)
    small_fresh_full = MOMENTUM * small_mom_full + small_grad

    def own_part(array):
        split = array.reshape(array.shape[0], dp_count, rows_here)
        return lax.dynamic_index_in_dim(split, me, 1, keepdims=False)

    small_grad_here = own_part(small_grad)
    small_fresh = MOMENTUM * small_mom + small_grad_here
    fresh_vectors = small_fresh[0:4]
    vector_scale = jnp.sqrt(
        jnp.mean(small_fresh_full[0:4] * small_fresh_full[0:4], axis=1, keepdims=True) + 1e-05
    )
    new_vectors = small[0:4] - VEC_RATE * fresh_vectors / vector_scale
    route_full = small_fresh_full[4:]
    route_factor = polar_factor(dot_high("ed,fd->ef", route_full, route_full))
    iterate_route = dot_high("er,ef->rf", small_fresh[4:], route_factor)
    route_rate = MAT_RATE * max(1.0, width / experts) ** 0.5
    new_router = router_weight - route_rate * iterate_route
    router_grad = small_grad_here[4:].T
    fresh_route = small_fresh[4:].T

    attn_rate = MAT_RATE * max(1.0, width / head_cols) ** 0.5
    fresh_attn = MOMENTUM * jnp.concatenate([qkv_mom, out_mom[None]], axis=0) + attn_grad
    new_attn = jnp.concatenate([qkv_weight, out_weight[None]], axis=0) - attn_rate * attn_iterate

    expert_rate = MAT_RATE * max(1.0, width / block_cols) ** 0.5

    def expert_step(weight, moment, grad):
        fresh = MOMENTUM * moment + grad
        expert_factor = polar_factor(dot_high("rq,rp->qp", fresh, fresh))
        return weight - expert_rate * dot_high("rq,qp->rp", fresh, expert_factor), fresh

    new_up, fresh_up = expert_step(expert_up[0], up_mom[0], up_grad_block)
    new_down, fresh_down = expert_step(expert_down[0], down_mom[0], down_grad_block)
    return (
        block_out,
        input_grad,
        small_grad_here[0:2],
        small_grad_here[2:4],
        attn_grad[0:3],
        attn_grad[3],
        router_grad,
        up_grad_block[None],
        down_grad_block[None],
        new_vectors[0:2],
        new_vectors[2:4],
        new_attn[0:3],
        new_attn[3],
        new_router,
        new_up[None],
        new_down[None],
        fresh_vectors[0:2],
        fresh_vectors[2:4],
        fresh_attn[0:3],
        fresh_attn[3],
        fresh_route,
        fresh_up[None],
        fresh_down[None],
    )


def body_slots(
    x_in,
    cotangent,
    routes,
    norm_gains,
    norm_biases,
    qkv_weight,
    out_weight,
    router_weight,
    expert_up,
    expert_down,
    gains_mom,
    biases_mom,
    qkv_mom,
    out_mom,
    router_mom,
    up_mom,
    down_mom,
):
    bf16 = jnp.bfloat16
    token_count = x_in.shape[0]
    images = token_count // SEQ
    experts = router_weight.shape[1]
    head_cols = qkv_weight.shape[2]
    heads_here = head_cols // DH
    capacity = 2 * min(token_count // 2, (2 * token_count + experts - 1) // experts)
    slots_all = experts * capacity
    gain_full, shift_full, weight_qkv, weight_out, weight_route = (
        lax.all_gather(norm_gains.astype(bf16), "dp", axis=1, tiled=True),
        lax.all_gather(norm_biases.astype(bf16), "dp", axis=1, tiled=True),
        lax.all_gather(qkv_weight.astype(bf16), "dp", axis=1, tiled=True),
        lax.all_gather(out_weight.astype(bf16), "dp", axis=0, tiled=True),
        lax.all_gather(router_weight.astype(bf16), "dp", axis=0, tiled=True),
    )
    gain_full = gain_full.astype(jnp.float32)
    shift_full = shift_full.astype(jnp.float32)
    weight_up = expert_up[0].astype(bf16)
    weight_down = expert_down[0].astype(bf16)
    inputs = x_in.astype(jnp.float32)
    normed_a, hat_a, scale_a = norm_forward(inputs, gain_full[0], shift_full[0])
    normed_a_bf = normed_a.astype(bf16)
    projected = jnp.einsum(
        "rd,jde->jre", normed_a_bf, weight_qkv, preferred_element_type=jnp.float32
    ).astype(bf16)
    split_heads = projected.reshape(3, images, SEQ, heads_here, DH)
    query, keys, values = (split_heads[0], split_heads[1], split_heads[2])
    score_scale = DH ** (-0.5)
    scores = (
        jnp.einsum("ishd,ithd->ihst", query, keys, preferred_element_type=jnp.float32) * score_scale
    )
    log_total = jnp.log(jnp.sum(jnp.exp(scores), axis=-1, keepdims=True))
    weights_bf = jnp.exp(scores - log_total).astype(bf16)
    context = jnp.einsum(
        "ihst,ithd->ishd", weights_bf, values, preferred_element_type=jnp.float32
    ).astype(bf16)
    context_rows = context.reshape(token_count, head_cols)
    attn_part = jnp.einsum(
        "rq,dq->rd", context_rows, weight_out, preferred_element_type=jnp.float32
    )
    attended = lax.psum(attn_part, "tensor")
    middle = inputs + attended
    normed_b, hat_b, scale_b = norm_forward(middle, gain_full[1], shift_full[1])
    normed_b_bf = normed_b.astype(bf16)
    logits = jnp.dot(normed_b_bf, weight_route, preferred_element_type=jnp.float32)
    expo = jnp.exp(logits)
    probs = expo / jnp.sum(expo, axis=-1, keepdims=True)
    chosen = (routes[:, :, None] == jnp.arange(experts, dtype=jnp.int32)[None, None, :]).astype(
        jnp.float32
    )
    picked = jnp.sum(chosen * probs[:, None, :], axis=-1)
    picked_total = jnp.sum(picked, axis=-1, keepdims=True)
    gates = picked / picked_total
    flat_routes = routes.reshape(-1)
    hot_counts = (flat_routes[:, None] == jnp.arange(experts, dtype=jnp.int32)[None, :]).astype(
        jnp.int32
    )
    earlier = jnp.cumsum(hot_counts, axis=0) - hot_counts
    position = jnp.sum(earlier * hot_counts, axis=1)
    slot_index = flat_routes * capacity + position
    placing = (slot_index[None, :] == jnp.arange(slots_all, dtype=jnp.int32)[:, None]).astype(bf16)
    repeated = jnp.repeat(normed_b_bf, 2, axis=0)
    dispatched = jnp.dot(placing, repeated, preferred_element_type=jnp.float32).astype(bf16)
    width = dispatched.shape[1]

    def deliver(buffer):
        sending = jnp.broadcast_to(
            buffer.reshape(experts, 1, capacity, width), (experts, 2, capacity, width)
        ).reshape(2 * experts, capacity, width)
        return lax.all_to_all(sending, "dp", split_axis=0, concat_axis=0, tiled=True)

    def collect(partial_value):
        returned = lax.all_to_all(partial_value, "dp", split_axis=0, concat_axis=0, tiled=True)
        return jnp.sum(
            returned.reshape(experts, 2, capacity, width).astype(jnp.float32), axis=1
        ).reshape(slots_all, width)

    token_block = deliver(dispatched).reshape(-1, width)
    pre_hidden = jnp.dot(token_block, weight_up, preferred_element_type=jnp.float32)
    hidden_bf = gelu_value(pre_hidden).astype(bf16)
    expert_part = jnp.einsum(
        "mb,db->md", hidden_bf, weight_down, preferred_element_type=jnp.float32
    ).astype(bf16)
    slot_values = collect(expert_part.reshape(2 * experts, capacity, width))
    per_route = jnp.take(slot_values, slot_index, axis=0).reshape(token_count, 2, width)
    mixed_part = jnp.sum(gates[:, :, None] * per_route, axis=1)
    mixed = lax.psum(mixed_part.astype(jnp.bfloat16), "tensor").astype(jnp.float32)
    block_out = (middle + mixed).astype(bf16)
    upstream = cotangent.astype(jnp.float32)
    gate_grad = jnp.sum(upstream[:, None, :] * per_route, axis=-1)
    route_values = (
        (gates[:, :, None] * upstream[:, None, :]).astype(bf16).reshape(2 * token_count, width)
    )
    slot_grads = jnp.dot(placing, route_values, preferred_element_type=jnp.float32).astype(bf16)
    grad_block = deliver(slot_grads).reshape(-1, width)
    hidden_grad = jnp.dot(grad_block, weight_down, preferred_element_type=jnp.float32)
    down_grad_block = jnp.einsum(
        "md,mb->db", grad_block, hidden_bf, preferred_element_type=jnp.float32
    )
    pre_grad_bf = (hidden_grad * gelu_slope(pre_hidden)).astype(bf16)
    up_grad_block = jnp.einsum(
        "md,mb->db", token_block, pre_grad_bf, preferred_element_type=jnp.float32
    )
    token_grad_part = jnp.einsum(
        "mb,db->md", pre_grad_bf, weight_up, preferred_element_type=jnp.float32
    ).astype(bf16)
    slot_back = collect(token_grad_part.reshape(2 * experts, capacity, width))
    expert_input_grad = jnp.sum(
        jnp.take(slot_back, slot_index, axis=0).reshape(token_count, 2, width), axis=1
    )
    weighted = jnp.sum(gate_grad * gates, axis=-1, keepdims=True)
    picked_grad = (gate_grad - weighted) / picked_total
    prob_grad = jnp.sum(chosen * picked_grad[:, :, None], axis=1)
    logit_grad = probs * (prob_grad - jnp.sum(probs * prob_grad, axis=-1, keepdims=True))
    route_grad_part = jnp.dot(normed_b_bf.astype(jnp.float32).T, logit_grad, precision=HIGHEST)
    normed_b_part = expert_input_grad + jnp.dot(
        logit_grad, weight_route.astype(jnp.float32).T, precision=HIGHEST
    )
    normed_b_grad, route_grad_full = lax.psum((normed_b_part, route_grad_part), "tensor")
    gain_b_grad = jnp.sum(normed_b_grad * hat_b, axis=0)
    shift_b_grad = jnp.sum(normed_b_grad, axis=0)
    middle_grad = upstream + norm_backward(normed_b_grad, hat_b, scale_b, gain_full[1])
    middle_grad_bf = middle_grad.astype(bf16)
    context_grad = jnp.dot(middle_grad_bf, weight_out, preferred_element_type=jnp.float32).astype(
        bf16
    )
    out_grad_part = jnp.einsum(
        "rd,rq->dq", middle_grad_bf, context_rows, preferred_element_type=jnp.float32
    )
    context_grad4 = context_grad.reshape(images, SEQ, heads_here, DH)
    scores_again = (
        jnp.einsum("ishd,ithd->ihst", query, keys, preferred_element_type=jnp.float32) * score_scale
    )
    probs_again = jnp.exp(scores_again - log_total)
    value_grad = jnp.einsum(
        "ihst,ishd->ithd",
        probs_again.astype(bf16),
        context_grad4,
        preferred_element_type=jnp.float32,
    ).astype(bf16)
    prob_grad_att = jnp.einsum(
        "ishd,ithd->ihst", context_grad4, values, preferred_element_type=jnp.float32
    )
    row_dot = jnp.einsum(
        "ishd,ishd->ihs", context_grad4, context, preferred_element_type=jnp.float32
    )[..., None]
    score_grad = (probs_again * (prob_grad_att - row_dot) * score_scale).astype(bf16)
    query_grad = jnp.einsum(
        "ihst,ithd->ishd", score_grad, keys, preferred_element_type=jnp.float32
    ).astype(bf16)
    key_grad = jnp.einsum(
        "ihst,ishd->ithd", score_grad, query, preferred_element_type=jnp.float32
    ).astype(bf16)
    projected_grad = jnp.stack([query_grad, key_grad, value_grad]).reshape(
        3, token_count, head_cols
    )
    qkv_grad_part = jnp.einsum(
        "rd,jre->jde", normed_a_bf, projected_grad, preferred_element_type=jnp.float32
    )
    normed_a_part = jnp.einsum(
        "jre,jde->rd", projected_grad, weight_qkv, preferred_element_type=jnp.float32
    )
    normed_a_grad = lax.psum(normed_a_part.astype(jnp.bfloat16), "tensor").astype(jnp.float32)
    gain_a_grad = jnp.sum(normed_a_grad * hat_a, axis=0)
    shift_a_grad = jnp.sum(normed_a_grad, axis=0)
    input_grad = (middle_grad + norm_backward(normed_a_grad, hat_a, scale_a, gain_full[0])).astype(
        bf16
    )
    gains_grad, biases_grad, qkv_grad, out_grad, router_grad = (
        lax.psum_scatter(
            jnp.stack([gain_a_grad, gain_b_grad]), "dp", scatter_dimension=1, tiled=True
        ),
        lax.psum_scatter(
            jnp.stack([shift_a_grad, shift_b_grad]), "dp", scatter_dimension=1, tiled=True
        ),
        lax.psum_scatter(qkv_grad_part, "dp", scatter_dimension=1, tiled=True),
        lax.psum_scatter(out_grad_part, "dp", scatter_dimension=0, tiled=True),
        lax.psum_scatter(route_grad_full, "dp", scatter_dimension=0, tiled=True),
    )
    fresh_attn = MOMENTUM * jnp.concatenate([qkv_mom, out_mom[None]], axis=0) + jnp.concatenate(
        [qkv_grad, out_grad[None]], axis=0
    )
    fresh_route = MOMENTUM * router_mom + router_grad
    fresh_vectors = MOMENTUM * jnp.concatenate([gains_mom, biases_mom], axis=0) + jnp.concatenate(
        [gains_grad, biases_grad], axis=0
    )
    square_vectors = lax.psum(jnp.sum(fresh_vectors * fresh_vectors, axis=1), "dp")
    dp_count = lax.axis_size("dp")
    rows_here = fresh_route.shape[0]
    spread = max(head_cols, experts)
    padded_route = jnp.pad(fresh_route, ((0, 0), (0, spread - experts)))[None]
    sending = jnp.concatenate(
        [fresh_attn, padded_route, jnp.zeros((dp_count - 5, rows_here, spread), jnp.float32)],
        axis=0,
    )
    owned = lax.all_to_all(sending, "dp", split_axis=0, concat_axis=0, tiled=True).reshape(
        1, dp_count * rows_here, spread
    )
    settled = orthogonalize(owned).reshape(dp_count, rows_here, spread)
    returned = lax.all_to_all(
        settled.astype(jnp.bfloat16), "dp", split_axis=0, concat_axis=0, tiled=True
    ).astype(settled.dtype)
    iterate_attn = returned[0:4, :, :head_cols]
    iterate_route = returned[4:5, :, :experts]
    attn_rate = MAT_RATE * max(1.0, D / head_cols) ** 0.5
    route_rate = MAT_RATE * max(1.0, D / experts) ** 0.5
    new_attn = jnp.concatenate([qkv_weight, out_weight[None]], axis=0) - attn_rate * iterate_attn
    new_router = router_weight - route_rate * iterate_route[0]
    vector_scale = jnp.sqrt(square_vectors / D + 1e-05)[:, None]
    new_vectors = (
        jnp.concatenate([norm_gains, norm_biases], axis=0) - VEC_RATE * fresh_vectors / vector_scale
    )
    fresh_experts = MOMENTUM * jnp.stack([up_mom[0], down_mom[0]]) + jnp.stack(
        [up_grad_block, down_grad_block]
    )
    expert_rate = MAT_RATE * max(1.0, D / weight_up.shape[1]) ** 0.5
    new_experts = jnp.stack([expert_up[0], expert_down[0]]) - expert_rate * orthogonalize(
        fresh_experts
    )
    return (
        block_out,
        input_grad,
        gains_grad,
        biases_grad,
        qkv_grad,
        out_grad,
        router_grad,
        up_grad_block[None],
        down_grad_block[None],
        new_vectors[0:2],
        new_vectors[2:4],
        new_attn[0:3],
        new_attn[3],
        new_router,
        new_experts[0:1],
        new_experts[1:2],
        fresh_vectors[0:2],
        fresh_vectors[2:4],
        fresh_attn[0:3],
        fresh_attn[3],
        fresh_route,
        fresh_experts[0:1],
        fresh_experts[1:2],
    )


def body(*arrays):
    token_count = arrays[0].shape[0]
    experts = arrays[7].shape[1]
    capacity = 2 * min(token_count // 2, (2 * token_count + experts - 1) // experts)
    line = lax.axis_size("dp") // 2
    dense = token_count <= 2 * capacity and line == experts and experts >= 4
    dense = dense and line & (line - 1) == 0 and lax.axis_size("tensor") == 4
    return (body_lines if dense else body_slots)(*arrays)


def solution(mesh):
    placed = (
        P("dp", None),
        P("dp", None),
        P("dp", None),
        P(None, "dp"),
        P(None, "dp"),
        P(None, "dp", "tensor"),
        P("dp", "tensor"),
        P("dp", None),
        P("dp", None, "tensor"),
        P("dp", None, "tensor"),
        P(None, "dp"),
        P(None, "dp"),
        P(None, "dp", "tensor"),
        P("dp", "tensor"),
        P("dp", None),
        P("dp", None, "tensor"),
        P("dp", None, "tensor"),
    )
    return jax.shard_map(
        body,
        mesh=mesh,
        in_specs=placed,
        out_specs=(
            P("dp", None),
            P("dp", None),
            P(None, "dp"),
            P(None, "dp"),
            P(None, "dp", "tensor"),
            P("dp", "tensor"),
            P("dp", None),
            P("dp", None, "tensor"),
            P("dp", None, "tensor"),
            P(None, "dp"),
            P(None, "dp"),
            P(None, "dp", "tensor"),
            P("dp", "tensor"),
            P("dp", None),
            P("dp", None, "tensor"),
            P("dp", None, "tensor"),
            P(None, "dp"),
            P(None, "dp"),
            P(None, "dp", "tensor"),
            P("dp", "tensor"),
            P("dp", None),
            P("dp", None, "tensor"),
            P("dp", None, "tensor"),
        ),
        check_vma=False,
    )
```
